32 devices in a mesh: panel: 2 (over y), gx: 16 (over z, x, core).
Axes of the slice: x: 2, y: 2, z: 4, core: 2. Of those that a mesh axis runs over, the one named last changes fastest.
Arguments:
- right_side: float32 [20, 1024, 256], P(None, 'gx', 'panel'), may hold values from -40 to 40
- previous: float32 [20, 1024, 256], P(None, 'gx', 'panel'), may hold values from -1.8 to 1.8
- diagonal: float32 [20, 1024, 256], P(None, 'gx', 'panel'), may hold values from 0.5 to 2
- vertical: float32 [19, 1024, 256], P(None, 'gx', 'panel'), may hold values from 0.5 to 2
- metric_a: float32 [1024, 256], P('gx', 'panel'), may hold values from 0.5 to 2
- metric_b: float32 [1024, 256], P('gx', 'panel'), may hold values from 0.5 to 2
- profile: float32 [20], replicated, may hold values from 0.5 to 2
- column_inverse: bfloat16 [4, 20, 1024, 256], P(None, None, 'gx', 'panel'), may hold values from -0.125 to 0.625, as said below
- edge_turn: int32 [4, 16, 2], replicated, may hold values from 0 to 3
Outputs:
- increment: float32 [20, 1024, 256], P(None, 'gx', 'panel')
The draws below stay inside these ranges and needn't reach their ends.
Inputs may be any that keep to these rules, and one draw needn't show every extreme that they name: Entry column_inverse[c, k] lies in row k mod 4, column c of the inverse of the block of 4 levels that holds level k. `edge_turn`: entries 0 and 2 are read only for their lowest bit; entries 1 and 3 reverse with the lowest bit and negate with the value 2 bit.
All inputs are finite; a program needn't handle non-finite values.
Results may differ from the reference program's by a relative error of at most 0.0003.
Values sent between devices are 32-bit elements; how exact they have to be, the bound alone decides.
A program may use at most 64 MiB of HBM per device.

```python
import math
import jax
import jax.numpy as jnp

LEVELS = 20
BK = 4
TA = 64
TB = 128
NA = 1024
NB = 256
N_PANEL = 2
N_GX = 16


def draw_right_side(key, part):
    key_rough = jax.random.fold_in(key, 0)
    ramp = 1.0 + 2.0 * jnp.arange(NA, dtype=jnp.float32)[None, :, None] / NA
    rough = jnp.clip(jax.random.normal(key_rough, (LEVELS, NA, NB), jnp.float32), -6.0, 6.0)
    return rough * ramp


def draw_column_inverse(key, part):
    key_diag, key_off = jax.random.split(key)
    full_shape = (BK, LEVELS, NA, NB)
    within = jnp.arange(LEVELS) % BK
    on_diag = (jnp.arange(BK)[:, None] == within[None, :])[:, :, None, None]
    diag_part = 0.2 * jnp.exp(jnp.log(3.0) * jax.random.uniform(key_diag, full_shape, jnp.float32))
    off_part = jax.random.uniform(key_off, full_shape, jnp.float32, -0.12, 0.12)
    return jnp.where(on_diag, diag_part, off_part).astype(jnp.bfloat16)


def with_ends(values, key, least, top_value):
    spot = [jax.random.randint(jax.random.fold_in(key, axis), (), 0, length) for axis, length in enumerate(values.shape)]
    longest = values.shape.index(max(values.shape))
    beside = spot[:longest] + [(spot[longest] + 1) % values.shape[longest]] + spot[longest + 1:]
    return values.at[tuple(spot)].set(least).at[tuple(beside)].set(top_value)


def block_scale(rng, extent, cuts, smallest, top_value):
    factor_of = 1.0
    for axis_at, shards_of in cuts:
        heights = jax.random.uniform(jax.random.fold_in(jax.random.fold_in(rng, 6), axis_at), (shards_of,), jnp.float32, smallest / len(cuts), top_value / len(cuts))
        factor_of = factor_of * jnp.repeat(jnp.exp(heights), extent[axis_at] // shards_of).reshape((-1,) + (1,) * (len(extent) - 1 - axis_at))
    return factor_of


def bell_draw(stream_key, shape, deviation, bound, shards=(), held_as=jnp.bfloat16):
    drawn = jax.random.normal(stream_key, shape, jnp.float32) * deviation
    if len(shards) > 0:
        drawn = block_scale(stream_key, shape, shards, -0.22, 0.18) * drawn
    return jnp.clip(drawn, min=-bound, max=bound).astype(held_as)


def setup_inputs(seed: int = 0) -> dict:
    arg_keys = jax.random.split(jax.random.key(seed), 10)
    right_side = draw_right_side(jax.random.fold_in(arg_keys[9], 71), 0)
    previous = bell_draw(arg_keys[1], (LEVELS, NA, NB), 0.3, 1.8, ((1, 16), (2, 2)), jnp.float32)
    diagonal = jnp.clip(jnp.exp(math.log(2.0) - 1.3862944 * jax.random.uniform(arg_keys[2], (LEVELS, NA, NB), jnp.float32) ** block_scale(arg_keys[2], (LEVELS, NA, NB), ((1, 16), (2, 2)), -0.2, 0.2)), 0.5, 2.0)
    vertical = jnp.clip(jnp.exp(math.log(2.0) - 1.3862944 * jax.random.uniform(arg_keys[3], (LEVELS - 1, NA, NB), jnp.float32) ** block_scale(arg_keys[3], (LEVELS - 1, NA, NB), ((1, 16), (2, 2)), -0.2, 0.2)), 0.5, 2.0)
    metric_a = jnp.clip(jnp.exp(math.log(2.0) - 1.3862944 * jax.random.uniform(arg_keys[4], (NA, NB), jnp.float32) ** block_scale(arg_keys[4], (NA, NB), ((0, 16), (1, 2)), -0.2, 0.2)), 0.5, 2.0)
    metric_b = jnp.clip(jnp.exp(math.log(2.0) - 1.3862944 * jax.random.uniform(arg_keys[5], (NA, NB), jnp.float32) ** block_scale(arg_keys[5], (NA, NB), ((0, 16), (1, 2)), -0.2, 0.2)), 0.5, 2.0)
    profile = jnp.clip(jnp.exp(jax.random.uniform(arg_keys[6], (LEVELS,), jnp.float32, math.log(0.5), math.log(2.0))), 0.5, 2.0)
    column_inverse = draw_column_inverse(jax.random.fold_in(arg_keys[9], 71), 0)
    edge_turn = with_ends(jax.random.randint(arg_keys[8], (4, N_GX, N_PANEL), 0, 4), jax.random.fold_in(arg_keys[8], 1), 0, 3).astype(jnp.int32)
    return dict(right_side=right_side, previous=previous, diagonal=diagonal, vertical=vertical, metric_a=metric_a, metric_b=metric_b, profile=profile, column_inverse=column_inverse, edge_turn=edge_turn)


def flip_where(condition, values, dimension):
    return jnp.where(condition, jnp.flip(values, dimension), values)


def apply_operator(pressure, diagonal, vertical, face_a, face_b, edge_turn):
    tiles = pressure.reshape(LEVELS, N_GX, TA, N_PANEL, TB)
    low_a = jnp.roll(tiles[:, :, -1], 1, axis=1)
    low_a = flip_where((edge_turn[0] % 2 == 1)[None, :, :, None], low_a, 3)
    prev_a = jnp.concatenate([low_a[:, :, None], tiles[:, :, :-1]], axis=2)
    low_b = jnp.roll(tiles[..., -1], 1, axis=3)
    low_b = flip_where((edge_turn[2] % 2 == 1)[None, :, None, :], low_b, 2)
    prev_b = jnp.concatenate([low_b[..., None], tiles[..., :-1]], axis=4)
    flux_a = face_a * (tiles - prev_a)
    flux_b = face_b * (tiles - prev_b)
    high_a = jnp.roll(flux_a[:, :, 0], -1, axis=1)
    turn_a = edge_turn[1][None, :, :, None]
    high_a = flip_where(turn_a % 2 == 1, high_a, 3)
    high_a = jnp.where(turn_a // 2 == 1, -high_a, high_a)
    next_a = jnp.concatenate([flux_a[:, :, 1:], high_a[:, :, None]], axis=2)
    high_b = jnp.roll(flux_b[..., 0], -1, axis=3)
    turn_b = edge_turn[3][None, :, None, :]
    high_b = flip_where(turn_b % 2 == 1, high_b, 2)
    high_b = jnp.where(turn_b // 2 == 1, -high_b, high_b)
    next_b = jnp.concatenate([flux_b[..., 1:], high_b[..., None]], axis=4)
    horizontal = (flux_a - next_a + flux_b - next_b).reshape(LEVELS, NA, NB)
    vertical_flux = vertical * (pressure[1:] - pressure[:-1])
    zeros_row = jnp.zeros((1, NA, NB), jnp.float32)
    upward = jnp.concatenate([zeros_row, vertical_flux], axis=0) - jnp.concatenate([vertical_flux, zeros_row], axis=0)
    return diagonal * pressure + horizontal + upward


def precondition(resid, column_inverse):
    blocks = resid.reshape(LEVELS // BK, BK, NA, NB)
    inverse = column_inverse.astype(jnp.float32).reshape(BK, LEVELS // BK, BK, NA, NB)
    result = inverse[0] * blocks[:, 0:1]
    for column in range(1, BK):
        result = result + inverse[column] * blocks[:, column:column + 1]
    return result.reshape(LEVELS, NA, NB)


def reference(right_side, previous, diagonal, vertical, metric_a, metric_b, profile, column_inverse, edge_turn):
    face_a = (metric_a[None] * profile[:, None, None]).reshape(LEVELS, N_GX, TA, N_PANEL, TB)
    face_b = (metric_b[None] * profile[:, None, None]).reshape(LEVELS, N_GX, TA, N_PANEL, TB)

    def operate(values):
        return apply_operator(values, diagonal, vertical, face_a, face_b, edge_turn)

    resid_first = right_side - operate(previous)
    search_first = precondition(resid_first, column_inverse)
    image_first = operate(search_first)
    square_first = jnp.sum(image_first * image_first)
    alpha_first = jnp.sum(resid_first * image_first) / square_first
    resid_second = resid_first - alpha_first * image_first
    search_second = precondition(resid_second, column_inverse)
    image_second = operate(search_second)
    beta_coef = jnp.sum(image_second * image_first) / square_first
    direction = search_second - beta_coef * search_first
    image_final = image_second - beta_coef * image_first
    alpha_second = jnp.sum(resid_second * image_final) / jnp.sum(image_final * image_final)
    return alpha_first * search_first + alpha_second * direction
```

```python
import functools

import jax
import jax.numpy as jnp
from jax import lax
from jax.experimental import pallas as pl
from jax.experimental.pallas import tpu as pltpu
from jax.sharding import PartitionSpec as P

BK = 4
PAD = 8
CH = 16
MESH = pl.DeviceIdType.MESH
F32 = jnp.float32


def rev_lanes(x):
    lanes = x.shape[1]
    index = lanes - 1 - lax.broadcasted_iota(jnp.int32, x.shape, 1)
    return jnp.take_along_axis(x, index, axis=1, mode="promise_in_bounds")


def rev_rows(x):
    rows = x.shape[0]
    parts = []
    for start in range(rows - 8, -1, -8):
        part = x[start : start + 8]
        index = 7 - lax.broadcasted_iota(jnp.int32, part.shape, 0)
        parts.append(jnp.take_along_axis(part, index, axis=0, mode="promise_in_bounds"))
    return jnp.concatenate(parts, axis=0)


def odd(code, shape):
    return jnp.full(shape, code & 1, jnp.int32) == 1


def sign_of(code, shape):
    return jnp.where(jnp.full(shape, code & 2, jnp.int32) == 2, -1.0, 1.0).astype(F32)


def kernel(
    n_panel, n_gx,
    right_h, prev_h, diag_h, vert_h, ma_h, mb_h, prof_s, inv_h, turn_s,
    out_ref,
    rs, pp, ss, ww, rr, qq, dg, vt, ma, mb, inv,
    sf, sl, sb, rl, rh, bl, bh, wpk, nma_v, nmb_v,
    row_out, row_in,
    in_sem, rf_send, rl_send, rl_recv, rh_recv, bu_send, bd_send, bl_recv, bh_recv,
    ar_send, ar_recv,
):
    levels, ta, tb = rs.shape
    n_dev = n_panel * n_gx
    g = lax.axis_index("gx")
    q = lax.axis_index("panel")
    me = q * n_gx + g
    g_next, g_prev = lax.rem(g + 1, n_gx), lax.rem(g + n_gx - 1, n_gx)
    q_next, q_prev = lax.rem(q + 1, n_panel), lax.rem(q + n_panel - 1, n_panel)
    one_pair = n_panel == 2

    loads = [
        pltpu.make_async_copy(prev_h, pp.at[:, pl.ds(PAD, ta), :], in_sem.at[0]),
        pltpu.make_async_copy(ma_h, ma.at[pl.ds(0, ta), :], in_sem.at[1]),
        pltpu.make_async_copy(mb_h, mb, in_sem.at[2]),
        pltpu.make_async_copy(diag_h, dg, in_sem.at[3]),
        pltpu.make_async_copy(vert_h, vt, in_sem.at[4]),
        pltpu.make_async_copy(right_h, rs, in_sem.at[5]),
        pltpu.make_async_copy(inv_h, inv, in_sem.at[6]),
    ]
    for load in loads:
        load.start()

    barrier = pltpu.get_barrier_semaphore()

    def greet(i, carry):
        other = lax.rem(me + i, n_dev)
        pl.semaphore_signal(
            barrier, inc=1, device_id=(other // n_gx, lax.rem(other, n_gx)), device_id_type=MESH
        )
        return carry

    lax.fori_loop(1, n_dev, greet, 0)

    t0, t1, t2, t3 = (turn_s[e, g, q] for e in range(4))
    t0n = turn_s[0, g_next, q]
    t2n = turn_s[2, g, q_next]
    rows_shape = sf.shape[1:]
    cols_shape = (ta, tb)

    ma[pl.ds(ta, 8), :] = jnp.ones((8, tb), F32)
    zeros_rows = jnp.zeros(rows_shape, F32)
    for j in range(3):
        sf[j] = zeros_rows
        sl[j] = zeros_rows

    lane = lax.broadcasted_iota(jnp.int32, (CH, tb), 1)
    pair = (lane - 1) >> 1
    lane_c = lax.broadcasted_iota(jnp.int32, cols_shape, 1)

    def remote(src, dst, send, recv, device):
        return pltpu.make_async_remote_copy(
            src_ref=src, dst_ref=dst, send_sem=send, recv_sem=recv,
            device_id=device, device_id_type=MESH,
        )

    def row_copies(j):
        return (
            remote(sl.at[j], rl.at[j], rl_send.at[j], rl_recv.at[j], (q, g_next)),
            remote(sf.at[j], rh.at[j], rf_send.at[j], rh_recv.at[j], (q, g_prev)),
        )

    def col_copies(j):
        down = remote(sb.at[j], bl.at[j], bu_send.at[j], bl_recv.at[j], (q_next, g))
        if one_pair:
            return (down,)
        return (down, remote(sb.at[j], bh.at[j], bd_send.at[j], bh_recv.at[j], (q_prev, g)))

    copies = []

    def send_rows(j, field):
        for k in range(levels):
            sf[j, pl.ds(k, 1), :] = field[k, pl.ds(PAD, 1), :]
            sl[j, pl.ds(k, 1), :] = field[k, pl.ds(PAD + ta - 1, 1), :]
        for copy in row_copies(j):
            copy.start()
            copies.append(copy)

    def send_cols(j):
        for copy in col_copies(j):
            copy.start()
            copies.append(copy)

    def pack(acc, value, k):
        return jnp.where(pair == k, pltpu.roll(value, 2 * k + 2, 1), acc)

    def receive(j, field):
        mine = sl[j]
        mine = jnp.where(odd(t0n, rows_shape), rev_lanes(mine), mine)
        mine_c = pltpu.roll(sb[j], 1, 1)
        mine_c = jnp.where(odd(t2n, cols_shape), rev_rows(mine_c), mine_c)
        for copy in col_copies(j):
            copy.wait_recv()
        from_low = bl[j]
        from_high = bl[j] if one_pair else bh[j]
        if j == 0:
            nmb_v[...] = jnp.broadcast_to(from_high[:, tb - 1 : tb], cols_shape)
        low_c = jnp.where(odd(t2, cols_shape), rev_rows(from_low), from_low)
        high_c = nmb_v[...] * (from_high - mine_c)
        high_c = jnp.where(odd(t3, cols_shape), rev_rows(high_c), high_c) * sign_of(t3, cols_shape)
        wpk[...] = jnp.where(lane_c & 1 == 1, low_c, pltpu.roll(high_c, tb - 2, 1))
        for copy in row_copies(j):
            copy.wait_recv()
        if j == 0:
            nma_v[...] = jnp.broadcast_to(rh[0, pl.ds(levels, 1), :], rows_shape)
        low = rl[j]
        low = jnp.where(odd(t0, rows_shape), rev_lanes(low), low)
        high = nma_v[...] * (rh[j] - mine)
        high = jnp.where(odd(t1, rows_shape), rev_lanes(high), high) * sign_of(t1, rows_shape)
        high = high + sl[j]
        for k in range(levels):
            field[k, pl.ds(PAD - 1, 1), :] = low[k : k + 1]
            field[k, pl.ds(PAD + ta, 1), :] = high[k : k + 1]

    def operate(field, c, emit):
        base = pl.multiple_of(c * CH, CH)
        at = pl.ds(base, CH)
        halo = wpk[at, :]
        ma_here = ma[at, :]
        ma_next = ma[pl.ds(base + 1, CH), :]
        mb_here = mb[at, :]
        below = None
        here = field[0, pl.ds(base + PAD, CH), :]
        for k in range(levels):
            before = field[k, pl.ds(base + PAD - 1, CH), :]
            after = field[k, pl.ds(base + PAD + 1, CH), :]
            edge = pltpu.roll(halo, (tb - 2 * k - 1) % tb, 1)
            left = jnp.where(lane == 0, edge, pltpu.roll(here, 1, 1))
            flux_b = mb_here * (here - left)
            next_b = jnp.where(lane == tb - 1, edge, pltpu.roll(flux_b, tb - 1, 1))
            flux = ma_here * (here - before) - ma_next * (after - here) + (flux_b - next_b)
            value = dg[k, at, :] * here + prof_s[k] * flux
            if below is not None:
                value = value + below
            if k + 1 < levels:
                above = field[k + 1, pl.ds(base + PAD, CH), :]
                vertical = vt[k, at, :] * (above - here)
                value = value - vertical
                below = vertical
            emit(k, here, value, at)
            if k + 1 < levels:
                here = above

    def precondition(block, start, at, store):
        results = []
        for k in range(BK):
            total = None
            for column in range(BK):
                term = inv[column, start + k, at, :].astype(F32) * block[column]
                total = term if total is None else total + term
            results.append(total)
        return results

    zero = jnp.zeros((CH, tb), F32)

    loads[0].wait()
    loads[1].wait()
    loads[2].wait()
    for k in range(1):
        sf[0, pl.ds(levels, 1), :] = ma[pl.ds(0, 1), :]

    def pack_previous(c, carry):
        base = pl.multiple_of(c * CH, CH)
        acc = pltpu.roll(mb[pl.ds(base, CH), :], tb - 1, 1)
        for k in range(levels):
            acc = pack(acc, pp[k, pl.ds(base + PAD, CH), :], k)
        sb[0, pl.ds(base, CH), :] = acc
        return carry

    pl.semaphore_wait(barrier, n_dev - 1)
    send_rows(0, pp)
    lax.fori_loop(0, ta // CH, pack_previous, 0)
    send_cols(0)
    for load in loads[3:]:
        load.wait()
    receive(0, pp)

    def first(c, carry):
        base = pl.multiple_of(c * CH, CH)
        state = {"block": [], "acc": zero}

        def emit(k, here, value, at):
            resid = rs[k, at, :] - value
            rr[k, at, :] = resid
            state["block"].append(resid)
            if len(state["block"]) == BK:
                start = k + 1 - BK
                for i, found in enumerate(precondition(state["block"], start, at, None)):
                    ss[start + i, pl.ds(base + PAD, CH), :] = found
                    state["acc"] = pack(state["acc"], found, start + i)
                state["block"] = []

        operate(pp, c, emit)
        sb[1, pl.ds(base, CH), :] = state["acc"]
        return carry

    lax.fori_loop(0, ta // CH, first, 0)
    send_cols(1)
    send_rows(1, ss)
    receive(1, ss)

    def second(c, carry):
        base = pl.multiple_of(c * CH, CH)
        state = {"block": [], "acc": zero, "rq": carry[0], "qq": carry[1]}

        def emit(k, here, value, at):
            qq[k, at, :] = value
            state["rq"] = state["rq"] + rr[k, at, :] * value
            state["qq"] = state["qq"] + value * value
            state["block"].append(value)
            if len(state["block"]) == BK:
                start = k + 1 - BK
                for i, found in enumerate(precondition(state["block"], start, at, None)):
                    ww[start + i, pl.ds(base + PAD, CH), :] = found
                    state["acc"] = pack(state["acc"], found, start + i)
                state["block"] = []

        operate(ss, c, emit)
        sb[2, pl.ds(base, CH), :] = state["acc"]
        return state["rq"], state["qq"]

    sum_rq, sum_qq = lax.fori_loop(0, ta // CH, second, (zero, zero))
    send_cols(2)
    send_rows(2, ww)
    receive(2, ww)

    def third(c, carry):
        state = {"rv": carry[0], "qv": carry[1], "vv": carry[2]}

        def emit(k, here, value, at):
            state["rv"] = state["rv"] + rr[k, at, :] * value
            state["qv"] = state["qv"] + qq[k, at, :] * value
            state["vv"] = state["vv"] + value * value

        operate(ww, c, emit)
        return state["rv"], state["qv"], state["vv"]

    sum_rv, sum_qv, sum_vv = lax.fori_loop(0, ta // CH, third, (zero, zero, zero))

    lane_1 = lax.broadcasted_iota(jnp.int32, (1, tb), 1)
    mine = jnp.zeros((1, tb), F32)
    for i, part in enumerate((sum_rq, sum_qq, sum_rv, sum_qv, sum_vv)):
        total = jnp.sum(jnp.sum(part, axis=0, keepdims=True), axis=1, keepdims=True)
        mine = jnp.where(lane_1 == i, total, mine)
    row_out[...] = mine

    def share(i, carry):
        other = lax.rem(me + i, n_dev)
        remote(
            row_out, row_in.at[i - 1], ar_send, ar_recv, (other // n_gx, lax.rem(other, n_gx))
        ).start()
        return carry

    lax.fori_loop(1, n_dev, share, 0)
    pltpu.make_async_copy(row_in, row_in, ar_recv).wait()
    sums = mine + jnp.sum(row_in[...], axis=0)

    rq, sq, rv, qv, vv = (sums[:, i : i + 1] for i in range(5))
    ratio = qv / sq
    weight = (rv - ratio * rq) / (vv - ratio * qv)
    on_search = jnp.broadcast_to(rq / sq - weight * ratio, (CH, tb))
    on_second = jnp.broadcast_to(weight, (CH, tb))

    def last(c, carry):
        base = pl.multiple_of(c * CH, CH)
        for k in range(levels):
            out_ref[k, pl.ds(base, CH), :] = (
                on_search * ss[k, pl.ds(base + PAD, CH), :]
                + on_second * ww[k, pl.ds(base + PAD, CH), :]
            )
        return carry

    lax.fori_loop(0, ta // CH, last, 0)
    for copy in copies:
        copy.wait_send()
    pltpu.make_async_copy(row_in, row_in, ar_send).wait()


def solution(mesh):
    n_panel, n_gx = mesh.shape["panel"], mesh.shape["gx"]
    n_dev = n_panel * n_gx

    def shards(right_side, previous, diagonal, vertical, metric_a, metric_b, profile, inverse, turn):
        levels, ta, tb = right_side.shape
        rows = (levels + 1 + 7) // 8 * 8
        vmem = pltpu.VMEM
        dma = pltpu.SemaphoreType.DMA
        field = vmem((levels, ta, tb), F32)
        padded = vmem((levels, ta + 2 * PAD, tb), F32)
        any_spec = pl.BlockSpec(memory_space=pl.ANY)
        smem_spec = pl.BlockSpec(memory_space=pltpu.SMEM)
        return pl.pallas_call(
            functools.partial(kernel, n_panel, n_gx),
            out_shape=jax.ShapeDtypeStruct((levels, ta, tb), F32),
            in_specs=[any_spec] * 6 + [smem_spec, any_spec, smem_spec],
            out_specs=pl.BlockSpec(memory_space=pltpu.VMEM),
            scratch_shapes=[
                field, padded, padded, padded, field, field, field,
                vmem((levels - 1, ta, tb), F32),
                vmem((ta + 8, tb), F32),
                vmem((ta, tb), F32),
                vmem((BK, levels, ta, tb), jnp.bfloat16),
                vmem((3, rows, tb), F32),
                vmem((3, rows, tb), F32),
                vmem((3, ta, tb), F32),
                vmem((3, rows, tb), F32),
                vmem((3, rows, tb), F32),
                vmem((3, ta, tb), F32),
                vmem((3, ta, tb), F32),
                vmem((ta, tb), F32),
                vmem((rows, tb), F32),
                vmem((ta, tb), F32),
                vmem((1, tb), F32),
                vmem((n_dev - 1, 1, tb), F32),
                dma((7,)), dma((3,)), dma((3,)), dma((3,)), dma((3,)),
                dma((3,)), dma((3,)), dma((3,)), dma((3,)),
                dma, dma,
            ],
            compiler_params=pltpu.CompilerParams(
                collective_id=0, has_side_effects=True, vmem_limit_bytes=32 * 1024 * 1024
            ),
        )(right_side, previous, diagonal, vertical, metric_a, metric_b, profile, inverse, turn)

    return jax.shard_map(
        shards,
        mesh=mesh,
        in_specs=(
            P(None, "gx", "panel"),
            P(None, "gx", "panel"),
            P(None, "gx", "panel"),
            P(None, "gx", "panel"),
            P("gx", "panel"),
            P("gx", "panel"),
            P(),
            P(None, None, "gx", "panel"),
            P(),
        ),
        out_specs=P(None, "gx", "panel"),
        check_vma=False,
    )
```

```python
import functools

import jax
import jax.numpy as jnp
from jax import lax
from jax.experimental import pallas as pl
from jax.experimental.pallas import tpu as pltpu
from jax.sharding import PartitionSpec as P

BK = 4
PAD = 8
CH = 16
MESH = pl.DeviceIdType.MESH
F32 = jnp.float32


def rev_lanes(x):
    lanes = x.shape[1]
    index = lanes - 1 - lax.broadcasted_iota(jnp.int32, x.shape, 1)
    return jnp.take_along_axis(x, index, axis=1, mode="promise_in_bounds")


def rev_rows(x):
    rows = x.shape[0]
    parts = []
    for start in range(rows - 8, -1, -8):
        part = x[start : start + 8]
        index = 7 - lax.broadcasted_iota(jnp.int32, part.shape, 0)
        parts.append(jnp.take_along_axis(part, index, axis=0, mode="promise_in_bounds"))
    return jnp.concatenate(parts, axis=0)


def odd(code, shape):
    return jnp.full(shape, code & 1, jnp.int32) == 1


def sign_of(code, shape):
    return jnp.where(jnp.full(shape, code & 2, jnp.int32) == 2, -1.0, 1.0).astype(F32)


def kernel(
    n_panel, n_gx,
    right_h, prev_h, diag_h, vert_h, ma_h, mb_h, prof_h, inv_h, turn_h,
    out_ref,
    rs, pp, ss, ww, rr, qq, dg, vt, ma, mb, inv,
    sf, sl, sb, rl, rh, bl, bh, wpk, nma_v, nmb_v,
    row_out, row_in,
    in_sem, rf_send, rl_send, rl_recv, rh_recv, bu_send, bd_send, bl_recv, bh_recv,
    ar_send, ar_recv, prof_s, turn_s,
):
    levels, ta, tb = rs.shape
    n_dev = n_panel * n_gx
    g = lax.axis_index("gx")
    q = lax.axis_index("panel")
    me = q * n_gx + g
    g_next, g_prev = lax.rem(g + 1, n_gx), lax.rem(g + n_gx - 1, n_gx)
    q_next, q_prev = lax.rem(q + 1, n_panel), lax.rem(q + n_panel - 1, n_panel)
    one_pair = n_panel == 2

    loads = [
        pltpu.make_async_copy(prev_h, pp.at[:, pl.ds(PAD, ta), :], in_sem.at[0]),
        pltpu.make_async_copy(ma_h, ma.at[pl.ds(0, ta), :], in_sem.at[1]),
        pltpu.make_async_copy(mb_h, mb, in_sem.at[2]),
        pltpu.make_async_copy(diag_h, dg, in_sem.at[3]),
        pltpu.make_async_copy(vert_h, vt, in_sem.at[4]),
        pltpu.make_async_copy(right_h, rs, in_sem.at[5]),
        pltpu.make_async_copy(inv_h, inv, in_sem.at[6]),
        pltpu.make_async_copy(prof_h, prof_s, in_sem.at[7]),
        pltpu.make_async_copy(turn_h, turn_s, in_sem.at[8]),
    ]
    for load in loads:
        load.start()

    barrier = pltpu.get_barrier_semaphore()

    def greet(i, carry):
        other = lax.rem(me + i, n_dev)
        pl.semaphore_signal(
            barrier, inc=1, device_id=(other // n_gx, lax.rem(other, n_gx)), device_id_type=MESH
        )
        return carry

    lax.fori_loop(1, n_dev, greet, 0)

    rows_shape = sf.shape[1:]
    cols_shape = (ta, tb)

    ma[pl.ds(ta, 8), :] = jnp.ones((8, tb), F32)
    zeros_rows = jnp.zeros(rows_shape, F32)
    for j in range(3):
        sf[j] = zeros_rows
        sl[j] = zeros_rows

    lane = lax.broadcasted_iota(jnp.int32, (CH, tb), 1)
    pair = (lane - 1) >> 1
    lane_c = lax.broadcasted_iota(jnp.int32, cols_shape, 1)

    def remote(src, dst, send, recv, device):
        return pltpu.make_async_remote_copy(
            src_ref=src, dst_ref=dst, send_sem=send, recv_sem=recv,
            device_id=device, device_id_type=MESH,
        )

    def row_copies(j):
        return (
            remote(sl.at[j], rl.at[j], rl_send.at[j], rl_recv.at[j], (q, g_next)),
            remote(sf.at[j], rh.at[j], rf_send.at[j], rh_recv.at[j], (q, g_prev)),
        )

    def col_copies(j):
        down = remote(sb.at[j], bl.at[j], bu_send.at[j], bl_recv.at[j], (q_next, g))
        if one_pair:
            return (down,)
        return (down, remote(sb.at[j], bh.at[j], bd_send.at[j], bh_recv.at[j], (q_prev, g)))

    copies = []

    def send_rows(j, field):
        for k in range(levels):
            sf[j, pl.ds(k, 1), :] = field[k, pl.ds(PAD, 1), :]
            sl[j, pl.ds(k, 1), :] = field[k, pl.ds(PAD + ta - 1, 1), :]
        for copy in row_copies(j):
            copy.start()
            copies.append(copy)

    def send_cols(j):
        for copy in col_copies(j):
            copy.start()
            copies.append(copy)

    def pack(acc, value, k):
        return jnp.where(pair == k, pltpu.roll(value, 2 * k + 2, 1), acc)

    def receive(j, field):
        mine = sl[j]
        mine = jnp.where(odd(t0n, rows_shape), rev_lanes(mine), mine)
        mine_c = pltpu.roll(sb[j], 1, 1)
        mine_c = jnp.where(odd(t2n, cols_shape), rev_rows(mine_c), mine_c)
        for copy in col_copies(j):
            copy.wait_recv()
        from_low = bl[j]
        from_high = bl[j] if one_pair else bh[j]
        if j == 0:
            nmb_v[...] = jnp.broadcast_to(from_high[:, tb - 1 : tb], cols_shape)
        low_c = jnp.where(odd(t2, cols_shape), rev_rows(from_low), from_low)
        high_c = nmb_v[...] * (from_high - mine_c)
        high_c = jnp.where(odd(t3, cols_shape), rev_rows(high_c), high_c) * sign_of(t3, cols_shape)
        wpk[...] = jnp.where(lane_c & 1 == 1, low_c, pltpu.roll(high_c, tb - 2, 1))
        for copy in row_copies(j):
            copy.wait_recv()
        if j == 0:
            nma_v[...] = jnp.broadcast_to(rh[0, pl.ds(levels, 1), :], rows_shape)
        low = rl[j]
        low = jnp.where(odd(t0, rows_shape), rev_lanes(low), low)
        high = nma_v[...] * (rh[j] - mine)
        high = jnp.where(odd(t1, rows_shape), rev_lanes(high), high) * sign_of(t1, rows_shape)
        high = high + sl[j]
        for k in range(levels):
            field[k, pl.ds(PAD - 1, 1), :] = low[k : k + 1]
            field[k, pl.ds(PAD + ta, 1), :] = high[k : k + 1]

    def operate(field, c, emit):
        base = pl.multiple_of(c * CH, CH)
        at = pl.ds(base, CH)
        halo = wpk[at, :]
        ma_here = ma[at, :]
        ma_next = ma[pl.ds(base + 1, CH), :]
        mb_here = mb[at, :]
        below = None
        here = field[0, pl.ds(base + PAD, CH), :]
        for k in range(levels):
            before = field[k, pl.ds(base + PAD - 1, CH), :]
            after = field[k, pl.ds(base + PAD + 1, CH), :]
            edge = pltpu.roll(halo, (tb - 2 * k - 1) % tb, 1)
            left = jnp.where(lane == 0, edge, pltpu.roll(here, 1, 1))
            flux_b = mb_here * (here - left)
            next_b = jnp.where(lane == tb - 1, edge, pltpu.roll(flux_b, tb - 1, 1))
            flux = ma_here * (here - before) - ma_next * (after - here) + (flux_b - next_b)
            value = dg[k, at, :] * here + prof_s[k] * flux
            if below is not None:
                value = value + below
            if k + 1 < levels:
                above = field[k + 1, pl.ds(base + PAD, CH), :]
                vertical = vt[k, at, :] * (above - here)
                value = value - vertical
                below = vertical
            emit(k, here, value, at)
            if k + 1 < levels:
                here = above

    def precondition(block, start, at, store):
        results = []
        for k in range(BK):
            total = None
            for column in range(BK):
                term = inv[column, start + k, at, :].astype(F32) * block[column]
                total = term if total is None else total + term
            results.append(total)
        return results

    zero = jnp.zeros((CH, tb), F32)

    loads[0].wait()
    loads[1].wait()
    loads[2].wait()
    for k in range(1):
        sf[0, pl.ds(levels, 1), :] = ma[pl.ds(0, 1), :]

    def pack_previous(c, carry):
        base = pl.multiple_of(c * CH, CH)
        acc = pltpu.roll(mb[pl.ds(base, CH), :], tb - 1, 1)
        for k in range(levels):
            acc = pack(acc, pp[k, pl.ds(base + PAD, CH), :], k)
        sb[0, pl.ds(base, CH), :] = acc
        return carry

    pl.semaphore_wait(barrier, n_dev - 1)
    send_rows(0, pp)
    lax.fori_loop(0, ta // CH, pack_previous, 0)
    send_cols(0)
    for load in loads[3:]:
        load.wait()
    t0, t1, t2, t3 = (turn_s[e, q, g] for e in range(4))
    t0n = turn_s[0, q, g_next]
    t2n = turn_s[2, q_next, g]
    receive(0, pp)

    def first(c, carry):
        base = pl.multiple_of(c * CH, CH)
        state = {"block": [], "acc": zero}

        def emit(k, here, value, at):
            resid = rs[k, at, :] - value
            rr[k, at, :] = resid
            state["block"].append(resid)
            if len(state["block"]) == BK:
                start = k + 1 - BK
                for i, found in enumerate(precondition(state["block"], start, at, None)):
                    ss[start + i, pl.ds(base + PAD, CH), :] = found
                    state["acc"] = pack(state["acc"], found, start + i)
                state["block"] = []

        operate(pp, c, emit)
        sb[1, pl.ds(base, CH), :] = state["acc"]
        return carry

    lax.fori_loop(0, ta // CH, first, 0)
    send_cols(1)
    send_rows(1, ss)
    receive(1, ss)

    def second(c, carry):
        base = pl.multiple_of(c * CH, CH)
        state = {"block": [], "acc": zero, "rq": carry[0], "qq": carry[1]}

        def emit(k, here, value, at):
            qq[k, at, :] = value
            state["rq"] = state["rq"] + rr[k, at, :] * value
            state["qq"] = state["qq"] + value * value
            state["block"].append(value)
            if len(state["block"]) == BK:
                start = k + 1 - BK
                for i, found in enumerate(precondition(state["block"], start, at, None)):
                    ww[start + i, pl.ds(base + PAD, CH), :] = found
                    state["acc"] = pack(state["acc"], found, start + i)
                state["block"] = []

        operate(ss, c, emit)
        sb[2, pl.ds(base, CH), :] = state["acc"]
        return state["rq"], state["qq"]

    sum_rq, sum_qq = lax.fori_loop(0, ta // CH, second, (zero, zero))
    send_cols(2)
    send_rows(2, ww)
    receive(2, ww)

    def third(c, carry):
        state = {"rv": carry[0], "qv": carry[1], "vv": carry[2]}

        def emit(k, here, value, at):
            state["rv"] = state["rv"] + rr[k, at, :] * value
            state["qv"] = state["qv"] + qq[k, at, :] * value
            state["vv"] = state["vv"] + value * value

        operate(ww, c, emit)
        return state["rv"], state["qv"], state["vv"]

    sum_rv, sum_qv, sum_vv = lax.fori_loop(0, ta // CH, third, (zero, zero, zero))

    lane_1 = lax.broadcasted_iota(jnp.int32, (1, tb), 1)
    mine = jnp.zeros((1, tb), F32)
    for i, part in enumerate((sum_rq, sum_qq, sum_rv, sum_qv, sum_vv)):
        total = jnp.sum(jnp.sum(part, axis=0, keepdims=True), axis=1, keepdims=True)
        mine = jnp.where(lane_1 == i, total, mine)
    row_out[...] = mine

    def share(i, carry):
        other = lax.rem(me + i, n_dev)
        remote(
            row_out, row_in.at[i - 1], ar_send, ar_recv, (other // n_gx, lax.rem(other, n_gx))
        ).start()
        return carry

    lax.fori_loop(1, n_dev, share, 0)
    pltpu.make_async_copy(row_in, row_in, ar_recv).wait()
    sums = mine + jnp.sum(row_in[...], axis=0)

    rq, sq, rv, qv, vv = (sums[:, i : i + 1] for i in range(5))
    ratio = qv / sq
    weight = (rv - ratio * rq) / (vv - ratio * qv)
    on_search = jnp.broadcast_to(rq / sq - weight * ratio, (CH, tb))
    on_second = jnp.broadcast_to(weight, (CH, tb))

    def last(c, carry):
        base = pl.multiple_of(c * CH, CH)
        for k in range(levels):
            out_ref[k, pl.ds(base, CH), :] = (
                on_search * ss[k, pl.ds(base + PAD, CH), :]
                + on_second * ww[k, pl.ds(base + PAD, CH), :]
            )
        return carry

    lax.fori_loop(0, ta // CH, last, 0)
    for copy in copies:
        copy.wait_send()
    pltpu.make_async_copy(row_in, row_in, ar_send).wait()


def solution(mesh):
    n_panel, n_gx = mesh.shape["panel"], mesh.shape["gx"]
    n_dev = n_panel * n_gx

    def shards(right_side, previous, diagonal, vertical, metric_a, metric_b, profile, inverse, turn):
        levels, ta, tb = right_side.shape
        rows = (levels + 1 + 7) // 8 * 8
        vmem = pltpu.VMEM
        dma = pltpu.SemaphoreType.DMA
        field = vmem((levels, ta, tb), F32)
        padded = vmem((levels, ta + 2 * PAD, tb), F32)
        any_spec = pl.BlockSpec(memory_space=pltpu.HBM)
        turn = jnp.transpose(turn, (0, 2, 1))
        return pl.pallas_call(
            functools.partial(kernel, n_panel, n_gx),
            out_shape=jax.ShapeDtypeStruct((levels, ta, tb), F32),
            in_specs=[any_spec] * 9,
            out_specs=pl.BlockSpec(memory_space=pltpu.VMEM),
            scratch_shapes=[
                field, padded, padded, padded, field, field, field,
                vmem((levels - 1, ta, tb), F32),
                vmem((ta + 8, tb), F32),
                vmem((ta, tb), F32),
                vmem((BK, levels, ta, tb), jnp.bfloat16),
                vmem((3, rows, tb), F32),
                vmem((3, rows, tb), F32),
                vmem((3, ta, tb), F32),
                vmem((3, rows, tb), F32),
                vmem((3, rows, tb), F32),
                vmem((3, ta, tb), F32),
                vmem((3, ta, tb), F32),
                vmem((ta, tb), F32),
                vmem((rows, tb), F32),
                vmem((ta, tb), F32),
                vmem((1, tb), F32),
                vmem((n_dev - 1, 1, tb), F32),
                dma((9,)), dma((3,)), dma((3,)), dma((3,)), dma((3,)),
                dma((3,)), dma((3,)), dma((3,)), dma((3,)),
                dma, dma,
                pltpu.SMEM(profile.shape, F32), pltpu.SMEM(turn.shape, jnp.int32),
            ],
            compiler_params=pltpu.CompilerParams(
                collective_id=0, has_side_effects=True, vmem_limit_bytes=60 * 1024 * 1024
            ),
        )(right_side, previous, diagonal, vertical, metric_a, metric_b, profile, inverse, turn)

    return jax.shard_map(
        shards,
        mesh=mesh,
        in_specs=(
            P(None, "gx", "panel"),
            P(None, "gx", "panel"),
            P(None, "gx", "panel"),
            P(None, "gx", "panel"),
            P("gx", "panel"),
            P("gx", "panel"),
            P(),
            P(None, None, "gx", "panel"),
            P(),
        ),
        out_specs=P(None, "gx", "panel"),
        check_vma=False,
    )
```
